32 devices in a mesh: band: 2 (over x), feed: 16 (over z, y, core).
Axes of the slice: x: 2, y: 2, z: 4, core: 2. Of those that a mesh axis runs over, the one named last changes fastest.
Arguments:
- samples: int32 [8192, 16, 519], P(('band', 'feed')), parts along dimension 0, may hold values from 0 to 255
- gains: int32 [2, 32, 4096], P(None, 'band', 'feed'), parts along dimension 1, may hold values from -2048 to 2047
- feed_slot: int32 [4096], replicated, may hold values from 0 to 4095, each once
Outputs:
- visibility: float32 [8192, 2, 4096], P(('band', 'feed')), parts along dimension 0
The draws below stay inside these ranges and needn't reach their ends.
There are 2 independent parts, one for each index of `band`. The reference program is written for one: setup_inputs(seed, part) draws one part's arguments, and reference() takes and returns one part's arrays. A program takes and returns all parts, laid end to end along the dimension named above; an argument that names none is the same for every part. Nothing has to cross between parts.
Inputs may be any that keep to these rules, and one draw needn't show every extreme that they name: `samples`: each word is 16 times the in-phase level plus the quadrature level, both offset by 8. `feed_slot`: every slot appears once.
All inputs are finite; a program needn't handle non-finite values.
Results may differ from the reference program's by a relative error of at most 0.0026.
Values may be sent and summed in bfloat16 or wider, within the bound.
A program may use at most 128 MiB of HBM per device.

```python
import math
import jax
import jax.numpy as jnp
from jax import lax

INPUTS = 4096
CH = 16
TAPS = 8
SPECTRA = 512
ROWS = 256
QUARTS = 1
NFRAME = 519
N_FEED = 16


def place_ends(entries, own_key, smallest, top_value):
    longest = entries.shape.index(max(entries.shape))
    spots = []
    for shift in (0, 1):
        where = [jax.random.randint(jax.random.fold_in(own_key, axis), (), 0, length) for axis, length in enumerate(entries.shape)]
        where[longest] = (where[longest] + shift) % entries.shape[longest]
        spots.append(tuple(where))
    return entries.at[spots[0]].set(smallest).at[spots[1]].set(top_value)


def setup_inputs(seed: int = 0, part: int = 0) -> dict:
    streams_of = jax.random.split(jax.random.key(seed), 4)
    part_splits = jax.random.split(jax.random.fold_in(streams_of[3], part), 4)
    return {
        "samples": place_ends(jax.random.randint(part_splits[0], (INPUTS, CH, NFRAME), 0, 256), jax.random.fold_in(part_splits[0], 1), 0, 255).astype(jnp.int32),
        "gains": place_ends(jax.random.randint(part_splits[1], (2, CH, INPUTS), -2048, 2048), jax.random.fold_in(part_splits[1], 1), -2048, 2047).astype(jnp.int32),
        "feed_slot": jax.random.permutation(streams_of[2], INPUTS).astype(jnp.int32),
    }


def filter_taps():
    length = TAPS * CH
    place = jnp.arange(length).astype(jnp.float32)
    window = 0.5 - 0.5 * jnp.cos(2.0 * math.pi * place / (length - 1))
    return (jnp.sinc((place - 0.5 * (length - 1)) / CH) * window).reshape(TAPS, CH)

def dft_table():
    index = jnp.arange(CH, dtype=jnp.int32)
    phase = index[:, None] * index[None, :] % CH
    angle = phase.astype(jnp.float32) * (2.0 * math.pi / CH)
    cosine = jnp.cos(angle) / math.sqrt(CH)
    sine = jnp.sin(angle) / math.sqrt(CH)
    upper = jnp.stack([cosine, sine], axis=1)
    lower = jnp.stack([-sine, cosine], axis=1)
    return jnp.stack([upper, lower], axis=0)

def channelize(words, scales, blocks):
    inphase = (words // 16 - 8).astype(jnp.float32) * 0.125
    quadrature = (words % 16 - 8).astype(jnp.float32) * 0.125
    voltage = jnp.stack([inphase, quadrature], axis=1)
    taps = filter_taps()
    count = words.shape[2] - TAPS + 1
    filtered = taps[0][None, None, :, None] * voltage[:, :, :, 0:count]
    for tap in range(1, TAPS):
        filtered = filtered + taps[tap][None, None, :, None] * voltage[:, :, :, tap:tap + count]
    split = filtered.reshape(filtered.shape[0], 2, CH, blocks, count // blocks)
    channels = jnp.einsum('pcqk,nqkat->canpt', dft_table(), split, precision=lax.Precision.HIGHEST)
    gain = scales.astype(jnp.float32) * (1.0 / 2048.0)
    gain_real = gain[0][:, None, :, None]
    gain_imag = gain[1][:, None, :, None]
    real = channels[:, :, :, 0]
    imag = channels[:, :, :, 1]
    weighted = jnp.stack([gain_real * real - gain_imag * imag, gain_real * imag + gain_imag * real], axis=3)
    return weighted.astype(jnp.bfloat16)

def reference(samples, gains, feed_slot):
    width = INPUTS // N_FEED

    def one_tile(first):
        words = lax.dynamic_slice_in_dim(samples, first, width, 0)
        scales = lax.dynamic_slice_in_dim(gains, first, width, 2)
        return channelize(words, scales, 1)[:, 0]
    firsts = jnp.arange(N_FEED, dtype=jnp.int32) * width
    tiles = lax.map(one_tile, firsts)
    weighted = jnp.transpose(tiles, (1, 0, 2, 3, 4)).reshape(CH, INPUTS, 2 * SPECTRA)
    span = QUARTS * ROWS

    def one_channel(channel_block):
        ordered = jnp.take(channel_block, feed_slot, axis=0)
        feed_rows = ordered[:span]
        real = feed_rows[:, :SPECTRA]
        imag = feed_rows[:, SPECTRA:]
        left_side = jnp.stack([feed_rows, jnp.concatenate([imag, -real], axis=1)], axis=1)
        left_side = left_side.reshape(2 * span, 2 * SPECTRA)
        product = jnp.dot(left_side, ordered.T, preferred_element_type=jnp.float32)
        return product.reshape(span, 2, INPUTS) * (1.0 / SPECTRA)
    visibility = lax.map(one_channel, weighted)
    return visibility.reshape(N_FEED * ROWS, 2, INPUTS)
```

```python
import functools
import math

import jax
import jax.numpy as jnp
import numpy as np
from jax import lax
from jax.experimental import pallas as pl
from jax.experimental.pallas import tpu as pltpu
from jax.sharding import PartitionSpec as P

CH = 16
TAPS = 8
SPECTRA = 512
ROWS = 256
CHUNKS = 1
BLOCK = 16
TERMS = 3
LANES = 128


def filter_bank():
    length = TAPS * CH
    place = np.arange(length, dtype=np.float64)
    window = 0.5 - 0.5 * np.cos(2.0 * math.pi * place / (length - 1))
    taps = (np.sinc((place - 0.5 * (length - 1)) / CH) * window).reshape(TAPS, CH)
    index = np.arange(CH)
    angle = (index[:, None] * index[None, :] % CH) * (2.0 * math.pi / CH)
    cosine = np.cos(angle) / math.sqrt(CH)
    sine = np.sin(angle) / math.sqrt(CH)
    table = np.stack([np.stack([cosine, sine], 1), np.stack([-sine, cosine], 1)], 0)
    bank = table[:, :, None, :, :] * taps[None, None, :, None, :]
    bank = 0.125 * bank.reshape(2 * CH, TAPS * 2 * CH)
    terms = []
    for _ in range(TERMS):
        term = bank.astype(jnp.bfloat16)
        terms.append(term)
        bank = bank - term.astype(np.float64)
    return np.concatenate(terms, 0)


def channel_kernel(start, count, bank_ref, words_ref, gains_ref, out_ref, rows):
    bank = bank_ref[...]
    for n in range(BLOCK):
        words = words_ref[n]
        inphase = ((words >> 4) - 8).astype(jnp.float32).astype(jnp.bfloat16)
        quadrature = ((words & 15) - 8).astype(jnp.float32).astype(jnp.bfloat16)
        voltage = jnp.concatenate([inphase, quadrature], axis=0)
        shifted = [voltage[:, start + t : start + t + count] for t in range(TAPS)]
        stacked = jnp.concatenate(shifted, axis=0)
        parts = jnp.dot(bank, stacked, preferred_element_type=jnp.float32)
        total = parts[: 2 * CH]
        for term in range(1, TERMS):
            total = total + parts[2 * CH * term : 2 * CH * (term + 1)]
        for lane in range(count // LANES):
            piece = total[:, lane * LANES : (lane + 1) * LANES]
            rows[0, lane, n * CH : (n + 1) * CH, :] = piece[:CH]
            rows[1, lane, n * CH : (n + 1) * CH, :] = piece[CH:]
    gain = gains_ref[...].astype(jnp.float32) * (1.0 / 2048.0)
    for c in range(CH):
        gain_real = gain[0][:, c : c + 1]
        gain_imag = gain[1][:, c : c + 1]
        for lane in range(count // LANES):
            real = rows[0, lane, pl.ds(c, BLOCK, stride=CH), :]
            imag = rows[1, lane, pl.ds(c, BLOCK, stride=CH), :]
            place = lane * LANES
            upper = gain_real * real - gain_imag * imag
            lower = gain_real * imag + gain_imag * real
            out_ref[c, :, place : place + LANES] = upper.astype(jnp.bfloat16)
            out_ref[c, :, count + place : count + place + LANES] = lower.astype(jnp.bfloat16)


def channelize(words, gains, start, count):
    inputs, _, frames = words.shape
    bank = jnp.asarray(filter_bank())
    return pl.pallas_call(
        functools.partial(channel_kernel, start, count),
        out_shape=jax.ShapeDtypeStruct((CH, inputs, 2 * count), jnp.bfloat16),
        grid=(inputs // BLOCK,),
        in_specs=[
            pl.BlockSpec(bank.shape, lambda i: (0, 0)),
            pl.BlockSpec((BLOCK, CH, frames), lambda i: (i, 0, 0)),
            pl.BlockSpec((2, BLOCK, CH), lambda i: (0, i, 0)),
        ],
        out_specs=pl.BlockSpec((CH, BLOCK, 2 * count), lambda i: (0, i, 0)),
        scratch_shapes=[pltpu.VMEM((2, count // LANES, BLOCK * CH, LANES), jnp.float32)],
        cost_estimate=pl.CostEstimate(
            flops=2 * inputs * count * bank.shape[0] * bank.shape[1],
            bytes_accessed=4 * words.size + 4 * inputs * CH * count,
            transcendentals=0,
        ),
    )(bank, words, gains)


def body(samples, gains, feed_slot):
    groups = lax.axis_size("feed") // CH
    position = lax.axis_index("feed")
    first = position % groups * ROWS
    spectra = samples.shape[2] - TAPS + 1
    count = spectra // CHUNKS
    turned_gains = jnp.transpose(gains, (0, 2, 1))
    own = lax.dynamic_slice_in_dim(feed_slot, first, ROWS, 0)
    total = None
    for chunk in range(CHUNKS):
        weighted = channelize(samples, turned_gains, chunk * count, count)
        if groups > 1:
            copies = jnp.broadcast_to(weighted[:, None], (CH, groups) + weighted.shape[1:])
            weighted = copies.reshape((CH * groups,) + weighted.shape[1:])
        moved = lax.all_to_all(weighted, "feed", split_axis=0, concat_axis=0, tiled=True)
        flat = moved.reshape(moved.shape[0] * moved.shape[1], moved.shape[2])
        ordered = jnp.take(flat, feed_slot, axis=0, mode="clip")
        feed_rows = jnp.take(flat, own, axis=0, mode="clip") * (1.0 / spectra)
        real, imag = feed_rows[:, :count], feed_rows[:, count:]
        left = jnp.stack([feed_rows, jnp.concatenate([imag, -real], axis=1)], axis=1)
        product = jnp.einsum("rok,jk->roj", left, ordered, preferred_element_type=jnp.float32)
        total = product if total is None else total + product
    return total


def solution(mesh):
    return jax.shard_map(
        body,
        mesh=mesh,
        in_specs=(P(("band", "feed"), None, None), P(None, "band", "feed"), P()),
        out_specs=P(("band", "feed"), None, None),
        check_vma=False,
    )
```

```python
import functools
import math

import jax
import jax.numpy as jnp
import numpy as np
from jax import lax
from jax.experimental import pallas as pl
from jax.experimental.pallas import tpu as pltpu
from jax.sharding import PartitionSpec as P

CH = 16
TAPS = 8
SPECTRA = 512
ROWS = 256
CHUNKS = 4
SPAN = 32
TILE = 512
TERMS = 3
LANES = 128


def filter_bank():
    length = TAPS * CH
    place = np.arange(length, dtype=np.float64)
    window = 0.5 - 0.5 * np.cos(2.0 * math.pi * place / (length - 1))
    taps = (np.sinc((place - 0.5 * (length - 1)) / CH) * window).reshape(TAPS, CH)
    index = np.arange(CH)
    angle = (index[:, None] * index[None, :] % CH) * (2.0 * math.pi / CH)
    cosine = np.cos(angle) / math.sqrt(CH)
    sine = np.sin(angle) / math.sqrt(CH)
    table = np.stack([np.stack([cosine, sine], 1), np.stack([-sine, cosine], 1)], 0)
    bank = table[:, :, None, :, :] * taps[None, None, :, None, :]
    bank = 0.125 * bank.reshape(2 * CH, TAPS * 2 * CH)
    terms = []
    for _ in range(TERMS):
        term = bank.astype(jnp.bfloat16)
        terms.append(term)
        bank = bank - term.astype(np.float64)
    return np.concatenate(terms, 0)


def channel_kernel(bank_ref, words_ref, tail_ref, gains_ref, out_ref, voltage, rows):
    bank = bank_ref[...]
    span = out_ref.shape[2]

    def unpack(words):
        inphase = ((words >> 4) - 8).astype(jnp.float32).astype(jnp.bfloat16)
        quadrature = ((words & 15) - 8).astype(jnp.float32).astype(jnp.bfloat16)
        return jnp.concatenate([inphase, quadrature], axis=0)

    for m in range(span):
        voltage[m * 2 * CH : (m + 1) * 2 * CH, :] = unpack(words_ref[m])
    for m in range(TAPS - 1):
        place = (span + m) * 2 * CH
        voltage[place : place + 2 * CH, :] = unpack(tail_ref[m])
    gain = gains_ref[...].astype(jnp.float32) * (1.0 / 2048.0)
    for s in range(span):
        window = voltage[s * 2 * CH : (s + TAPS) * 2 * CH, :]
        parts = jnp.dot(bank, window, preferred_element_type=jnp.float32)
        total = parts[: 2 * CH]
        for term in range(1, TERMS):
            total = total + parts[2 * CH * term : 2 * CH * (term + 1)]
        real, imag = total[:CH], total[CH:]
        upper = gain[0] * real - gain[1] * imag
        lower = gain[0] * imag + gain[1] * real
        for lane in range(upper.shape[1] // LANES):
            place = slice(lane * LANES, (lane + 1) * LANES)
            rows[0, lane, s * CH : (s + 1) * CH, :] = upper[:, place]
            rows[1, lane, s * CH : (s + 1) * CH, :] = lower[:, place]
    for c in range(CH):
        for part in range(2):
            for lane in range(out_ref.shape[3] // LANES):
                place = slice(lane * LANES, (lane + 1) * LANES)
                piece = rows[part, lane, pl.ds(c, span, stride=CH), :]
                out_ref[c, part, :, place] = piece.astype(jnp.bfloat16)


def channelize(words, gains, start, count):
    inputs = words.shape[2]
    bank = jnp.asarray(filter_bank())
    span = min(SPAN, count)
    skip = start // span
    return pl.pallas_call(
        channel_kernel,
        out_shape=jax.ShapeDtypeStruct((CH, 2, count, inputs), jnp.bfloat16),
        grid=(count // span,),
        in_specs=[
            pl.BlockSpec(bank.shape, lambda i: (0, 0)),
            pl.BlockSpec((span, CH, inputs), lambda i: (skip + i, 0, 0)),
            pl.BlockSpec((8, CH, inputs), lambda i: ((skip + i + 1) * (span // 8), 0, 0)),
            pl.BlockSpec(gains.shape, lambda i: (0, 0, 0)),
        ],
        out_specs=pl.BlockSpec((CH, 2, span, inputs), lambda i: (0, 0, i, 0)),
        scratch_shapes=[
            pltpu.VMEM(((span + TAPS) * 2 * CH, inputs), jnp.bfloat16),
            pltpu.VMEM((2, inputs // LANES, span * CH, LANES), jnp.float32),
        ],
        cost_estimate=pl.CostEstimate(
            flops=2 * inputs * count * bank.shape[0] * bank.shape[1],
            bytes_accessed=4 * words.shape[1] * inputs * count + 4 * inputs * CH * count,
            transcendentals=0,
        ),
    )(bank, words, words, gains)


def product_kernel(scale, has_total, moved_ref, slot_ref, own_ref, *refs):
    out_ref, left = refs[-2], refs[-1]
    sources, depth, width = moved_ref.shape

    def pick(columns):
        total = None
        for source in range(sources):
            place = lax.broadcasted_iota(jnp.int32, (width, columns.shape[1]), 0) + source * width
            hot = jnp.where(place == columns, 1.0, 0.0).astype(jnp.bfloat16)
            part = jnp.dot(moved_ref[source], hot, preferred_element_type=jnp.float32)
            total = part if total is None else total + part
        return total

    @pl.when(pl.program_id(0) == 0)
    def _():
        feed_rows = jnp.transpose(pick(own_ref[...])) * scale
        real, imag = feed_rows[:, : depth // 2], feed_rows[:, depth // 2 :]
        left[0] = jnp.concatenate([real, imag], axis=1).astype(jnp.bfloat16)
        left[1] = jnp.concatenate([imag, -real], axis=1).astype(jnp.bfloat16)

    ordered = pick(slot_ref[...]).astype(jnp.bfloat16)
    for part in range(2):
        product = jnp.dot(left[part], ordered, preferred_element_type=jnp.float32)
        if has_total:
            product = product + refs[0][:, part, :]
        out_ref[:, part, :] = product


def correlate(moved, feed_slot, own, total, scale):
    sources, depth, width = moved.shape
    feeds = sources * width
    tile = min(TILE, feeds)
    block = pl.BlockSpec((ROWS, 2, tile), lambda j: (0, 0, j))
    return pl.pallas_call(
        functools.partial(product_kernel, scale, total is not None),
        out_shape=jax.ShapeDtypeStruct((ROWS, 2, feeds), jnp.float32),
        grid=(feeds // tile,),
        in_specs=[
            pl.BlockSpec(moved.shape, lambda j: (0, 0, 0)),
            pl.BlockSpec((1, tile), lambda j: (0, j)),
            pl.BlockSpec((1, ROWS), lambda j: (0, 0)),
        ]
        + ([] if total is None else [block]),
        out_specs=block,
        scratch_shapes=[pltpu.VMEM((2, ROWS, depth), jnp.bfloat16)],
        input_output_aliases={} if total is None else {3: 0},
        cost_estimate=pl.CostEstimate(
            flops=2 * depth * feeds * (feeds + 2 * ROWS),
            bytes_accessed=2 * moved.size + 8 * ROWS * feeds,
            transcendentals=0,
        ),
    )(moved, feed_slot[None], own[None], *([] if total is None else [total]))


def body(samples, gains, feed_slot):
    groups = lax.axis_size("feed") // CH
    position = lax.axis_index("feed")
    first = position % groups * ROWS
    inputs = samples.shape[0]
    spectra = samples.shape[2] - TAPS + 1
    count = spectra // CHUNKS
    words = jnp.transpose(samples, (2, 1, 0))
    spare = -inputs % LANES
    if spare:
        words = jnp.pad(words, ((0, 0), (0, 0), (0, spare)))
        gains = jnp.pad(gains, ((0, 0), (0, 0), (0, spare)))
    own = lax.dynamic_slice_in_dim(feed_slot, first, ROWS, 0)
    total = None
    for chunk in range(CHUNKS):
        weighted = channelize(words, gains, chunk * count, count)
        weighted = weighted.reshape(CH, 2 * count, inputs + spare)[:, :, :inputs]
        if groups > 1:
            copies = jnp.broadcast_to(weighted[:, None], (CH, groups) + weighted.shape[1:])
            weighted = copies.reshape((CH * groups,) + weighted.shape[1:])
        moved = lax.all_to_all(weighted, "feed", split_axis=0, concat_axis=0, tiled=True)
        total = correlate(moved, feed_slot, own, total, 1.0 / spectra)
    return total


def solution(mesh):
    return jax.shard_map(
        body,
        mesh=mesh,
        in_specs=(P(("band", "feed"), None, None), P(None, "band", "feed"), P()),
        out_specs=P(("band", "feed"), None, None),
        check_vma=False,
    )
```

```python
import functools
import math

import jax
import jax.numpy as jnp
import numpy as np
from jax import lax
from jax.experimental import pallas as pl
from jax.experimental.pallas import tpu as pltpu
from jax.sharding import PartitionSpec as P

CH = 16
TAPS = 8
SPECTRA = 512
ROWS = 256
SHARES = (4, 5, 5, 2)
SPAN = 32
TILE = 512
TERMS = 3
LANES = 128


def filter_bank():
    length = TAPS * CH
    place = np.arange(length, dtype=np.float64)
    window = 0.5 - 0.5 * np.cos(2.0 * math.pi * place / (length - 1))
    taps = (np.sinc((place - 0.5 * (length - 1)) / CH) * window).reshape(TAPS, CH)
    index = np.arange(CH)
    angle = (index[:, None] * index[None, :] % CH) * (2.0 * math.pi / CH)
    cosine = np.cos(angle) / math.sqrt(CH)
    sine = np.sin(angle) / math.sqrt(CH)
    table = np.stack([np.stack([cosine, sine], 1), np.stack([-sine, cosine], 1)], 0)
    bank = table[:, :, None, :, :] * taps[None, None, :, None, :]
    bank = 0.125 * bank.reshape(2 * CH, TAPS * 2 * CH)
    terms = []
    for _ in range(TERMS):
        term = bank.astype(jnp.bfloat16)
        terms.append(term)
        bank = bank - term.astype(np.float64)
    return np.concatenate(terms, 0)


def unpack(words):
    inphase = ((words >> 4) - 8).astype(jnp.float32).astype(jnp.bfloat16)
    quadrature = ((words & 15) - 8).astype(jnp.float32).astype(jnp.bfloat16)
    return jnp.concatenate([inphase, quadrature], axis=0)


def pick(moved_ref, columns):
    sources, _, width = moved_ref.shape
    total = None
    for source in range(sources):
        place = lax.broadcasted_iota(jnp.int32, (width, columns.shape[1]), 0) + source * width
        hot = jnp.where(place == columns, 1.0, 0.0).astype(jnp.bfloat16)
        part = jnp.dot(moved_ref[source], hot, preferred_element_type=jnp.float32)
        total = part if total is None else total + part
    return total


def set_left(left, moved_ref, columns, scale):
    depth = moved_ref.shape[1]
    feed_rows = jnp.transpose(pick(moved_ref, columns)) * scale
    real, imag = feed_rows[:, : depth // 2], feed_rows[:, depth // 2 :]
    left[0, :, :depth] = jnp.concatenate([real, imag], axis=1).astype(jnp.bfloat16)
    left[1, :, :depth] = jnp.concatenate([imag, -real], axis=1).astype(jnp.bfloat16)


def exchange_kernel(counts, groups, scale, bank_ref, words_hbm, gains_ref, slot_ref, own_ref, *refs):
    chunks = len(counts)
    last_hbm, total_hbm = refs[:2]
    words_bufs = refs[2 : 2 + chunks]
    send_bufs = refs[2 + chunks : 2 + 2 * chunks]
    hold_bufs = refs[2 + 2 * chunks : 1 + 3 * chunks]
    voltage, rows, total, left, word_sem, own_sem, total_sem, send_sem, recv_sem = refs[1 + 3 * chunks :]
    targets = hold_bufs + (last_hbm,)
    me = lax.axis_index("feed")
    size = lax.axis_size("feed")
    inputs = send_bufs[0].shape[2]
    bank = bank_ref[...]
    gain = gains_ref[...].astype(jnp.float32) * (1.0 / 2048.0)

    barrier = pltpu.get_barrier_semaphore()

    def greet(d, carry):
        pl.semaphore_signal(
            barrier, inc=1, device_id={"feed": (me + d) % size}, device_id_type=pl.DeviceIdType.MESH
        )
        return carry

    lax.fori_loop(1, size, greet, 0)

    def word_copy(k):
        source = words_hbm.at[pl.ds(sum(counts[:k]), counts[k] + TAPS - 1)]
        return pltpu.make_async_copy(source, words_bufs[k], word_sem.at[k])

    def own_copy(k):
        return pltpu.make_async_copy(send_bufs[k].at[me // groups], targets[k].at[me], own_sem.at[k])

    def remote(k, d):
        there = (me + d) % size
        return pltpu.make_async_remote_copy(
            src_ref=send_bufs[k].at[there // groups],
            dst_ref=targets[k].at[me],
            send_sem=send_sem.at[k, d],
            recv_sem=recv_sem.at[k, d],
            device_id={"feed": there},
            device_id_type=pl.DeviceIdType.MESH,
        )

    def channelize(k):
        words, out = words_bufs[k], send_bufs[k]
        count = counts[k]

        def block(i, carry):
            base = i * SPAN
            for m in range(SPAN + TAPS - 1):
                voltage[m * 2 * CH : (m + 1) * 2 * CH, :] = unpack(words[base + m])
            for s in range(SPAN):
                window = voltage[s * 2 * CH : (s + TAPS) * 2 * CH, :]
                parts = jnp.dot(bank, window, preferred_element_type=jnp.float32)
                whole = parts[: 2 * CH]
                for term in range(1, TERMS):
                    whole = whole + parts[2 * CH * term : 2 * CH * (term + 1)]
                real, imag = whole[:CH], whole[CH:]
                upper = gain[0] * real - gain[1] * imag
                lower = gain[0] * imag + gain[1] * real
                for lane in range(rows.shape[1]):
                    place = slice(lane * LANES, (lane + 1) * LANES)
                    rows[0, lane, s * CH : (s + 1) * CH, :] = upper[:, place]
                    rows[1, lane, s * CH : (s + 1) * CH, :] = lower[:, place]
            for c in range(CH):
                for part in range(2):
                    where = pl.ds(pl.multiple_of(part * count + base, SPAN), SPAN)
                    for lane in range(rows.shape[1]):
                        width = min(LANES, inputs - lane * LANES)
                        piece = rows[part, lane, pl.ds(c, SPAN, stride=CH), :]
                        out[c, where, lane * LANES : lane * LANES + width] = piece[:, :width].astype(
                            jnp.bfloat16
                        )
            return carry

        lax.fori_loop(0, count // SPAN, block, 0)

    def send(k):
        def one(d, carry):
            remote(k, d).start()
            return carry

        lax.fori_loop(1, size, one, 0)
        own_copy(k).start()

    def arrive(k):
        def one(d, carry):
            remote(k, d).wait_recv()
            return carry

        own_copy(k).wait()
        lax.fori_loop(1, size, one, 0)

    def drain(k):
        def one(d, carry):
            remote(k, d).wait_send()
            return carry

        lax.fori_loop(1, size, one, 0)

    for k in range(chunks):
        word_copy(k).start()
    for k in range(chunks):
        word_copy(k).wait()
        channelize(k)
        if k == 0:
            pl.semaphore_wait(barrier, size - 1)
        send(k)

    feeds = slot_ref.shape[1]
    tile = min(TILE, feeds)
    for k in range(chunks - 1):
        arrive(k)
        depth = 2 * counts[k]
        set_left(left, hold_bufs[k], own_ref[...], scale)

        def columns(j, carry, k=k, depth=depth):
            where = pl.ds(pl.multiple_of(j * tile, tile), tile)
            ordered = pick(hold_bufs[k], slot_ref[:, where]).astype(jnp.bfloat16)
            for part in range(2):
                product = jnp.dot(left[part, :, :depth], ordered, preferred_element_type=jnp.float32)
                if k:
                    product = product + total[part, :, where]
                total[part, :, where] = product
            return carry

        lax.fori_loop(0, feeds // tile, columns, 0)
    total_copy = pltpu.make_async_copy(total, total_hbm, total_sem)
    total_copy.start()
    arrive(chunks - 1)
    for k in range(chunks):
        drain(k)
    total_copy.wait()


def exchange(words, gains, feed_slot, own, counts, inputs, groups, scale):
    size = CH * groups
    feeds = feed_slot.shape[0]
    wide = words.shape[2]
    bank = jnp.asarray(filter_bank())
    held = [jax.ShapeDtypeStruct((size, 2 * count, inputs), jnp.bfloat16) for count in counts]
    memory = pl.BlockSpec(memory_space=pltpu.VMEM)
    anywhere = pl.BlockSpec(memory_space=pl.ANY)
    chunks = len(counts)
    return pl.pallas_call(
        functools.partial(exchange_kernel, counts, groups, scale),
        out_shape=(held[-1], jax.ShapeDtypeStruct((2, ROWS, feeds), jnp.float32)),
        in_specs=[memory, anywhere, memory, memory, memory],
        out_specs=(anywhere, anywhere),
        scratch_shapes=[pltpu.VMEM((count + TAPS - 1, CH, wide), jnp.int32) for count in counts]
        + [pltpu.VMEM((CH, 2 * count, inputs), jnp.bfloat16) for count in counts]
        + [pltpu.VMEM(one.shape, one.dtype) for one in held[:-1]]
        + [
            pltpu.VMEM(((SPAN + TAPS) * 2 * CH, wide), jnp.bfloat16),
            pltpu.VMEM((2, wide // LANES, SPAN * CH, LANES), jnp.float32),
            pltpu.VMEM((2, ROWS, feeds), jnp.float32),
            pltpu.VMEM((2, ROWS, 2 * max(counts)), jnp.bfloat16),
            pltpu.SemaphoreType.DMA((chunks,)),
            pltpu.SemaphoreType.DMA((chunks,)),
            pltpu.SemaphoreType.DMA,
            pltpu.SemaphoreType.DMA((chunks, size)),
            pltpu.SemaphoreType.DMA((chunks, size)),
        ],
        compiler_params=pltpu.CompilerParams(
            collective_id=0, has_side_effects=True, vmem_limit_bytes=60 * 2**20
        ),
    )(bank, words, gains, feed_slot[None], own[None])


def finish_kernel(scale, moved_ref, slot_ref, own_ref, total_ref, out_ref, left):
    @pl.when(pl.program_id(0) == 0)
    def _():
        set_left(left, moved_ref, own_ref[...], scale)

    ordered = pick(moved_ref, slot_ref[...]).astype(jnp.bfloat16)
    for part in range(2):
        product = jnp.dot(left[part], ordered, preferred_element_type=jnp.float32)
        out_ref[:, part, :] = product + total_ref[part]


def finish(moved, feed_slot, own, total, scale):
    feeds = feed_slot.shape[0]
    tile = min(TILE, feeds)
    return pl.pallas_call(
        functools.partial(finish_kernel, scale),
        out_shape=jax.ShapeDtypeStruct((ROWS, 2, feeds), jnp.float32),
        grid=(feeds // tile,),
        in_specs=[
            pl.BlockSpec(moved.shape, lambda j: (0, 0, 0)),
            pl.BlockSpec((1, tile), lambda j: (0, j)),
            pl.BlockSpec((1, ROWS), lambda j: (0, 0)),
            pl.BlockSpec((2, ROWS, tile), lambda j: (0, 0, j)),
        ],
        out_specs=pl.BlockSpec((ROWS, 2, tile), lambda j: (0, 0, j)),
        scratch_shapes=[pltpu.VMEM((2, ROWS, moved.shape[1]), jnp.bfloat16)],
    )(moved, feed_slot[None], own[None], total)


def body(samples, gains, feed_slot):
    groups = lax.axis_size("feed") // CH
    first = lax.axis_index("feed") % groups * ROWS
    inputs = samples.shape[0]
    spectra = samples.shape[2] - TAPS + 1
    counts = tuple(spectra * share // sum(SHARES) for share in SHARES)
    words = jnp.transpose(samples, (2, 1, 0))
    spare = -inputs % LANES
    if spare:
        words = jnp.pad(words, ((0, 0), (0, 0), (0, spare)))
        gains = jnp.pad(gains, ((0, 0), (0, 0), (0, spare)))
    own = lax.dynamic_slice_in_dim(feed_slot, first, ROWS, 0)
    scale = 1.0 / spectra
    moved, total = exchange(words, gains, feed_slot, own, counts, inputs, groups, scale)
    return finish(moved, feed_slot, own, total, scale)


def solution(mesh):
    return jax.shard_map(
        body,
        mesh=mesh,
        in_specs=(P(("band", "feed"), None, None), P(None, "band", "feed"), P()),
        out_specs=P(("band", "feed"), None, None),
        check_vma=False,
    )
```

```python
import functools
import math

import jax
import jax.numpy as jnp
import numpy as np
from jax import lax
from jax.experimental import pallas as pl
from jax.experimental.pallas import tpu as pltpu
from jax.sharding import PartitionSpec as P

CH = 16
TAPS = 8
SPECTRA = 512
ROWS = 256
SHARES = (4, 5, 5, 2)
SPAN = 32
TILE = 512
TERMS = 3
LANES = 128


def filter_bank():
    length = TAPS * CH
    place = np.arange(length, dtype=np.float64)
    window = 0.5 - 0.5 * np.cos(2.0 * math.pi * place / (length - 1))
    taps = (np.sinc((place - 0.5 * (length - 1)) / CH) * window).reshape(TAPS, CH)
    index = np.arange(CH)
    angle = (index[:, None] * index[None, :] % CH) * (2.0 * math.pi / CH)
    cosine = np.cos(angle) / math.sqrt(CH)
    sine = np.sin(angle) / math.sqrt(CH)
    table = np.stack([np.stack([cosine, sine], 1), np.stack([-sine, cosine], 1)], 0)
    bank = table[:, :, None, :, :] * taps[None, None, :, None, :]
    bank = 0.125 * bank.reshape(2 * CH, TAPS * 2 * CH)
    terms = []
    for _ in range(TERMS):
        term = bank.astype(jnp.bfloat16)
        terms.append(term)
        bank = bank - term.astype(np.float64)
    return np.concatenate(terms, 0)


def unpack(words):
    inphase = ((words >> 4) - 8).astype(jnp.float32).astype(jnp.bfloat16)
    quadrature = ((words & 15) - 8).astype(jnp.float32).astype(jnp.bfloat16)
    return jnp.concatenate([inphase, quadrature], axis=0)


def pick(moved_ref, columns):
    sources, _, width = moved_ref.shape
    total = None
    for source in range(sources):
        place = lax.broadcasted_iota(jnp.int32, (width, columns.shape[1]), 0) + source * width
        hot = jnp.where(place == columns, 1.0, 0.0).astype(jnp.bfloat16)
        part = jnp.dot(moved_ref[source], hot, preferred_element_type=jnp.float32)
        total = part if total is None else total + part
    return total


def set_left(left, feed_columns, scale):
    depth = feed_columns.shape[0]
    feed_rows = jnp.transpose(feed_columns) * scale
    real, imag = feed_rows[:, : depth // 2], feed_rows[:, depth // 2 :]
    left[0, :, :depth] = jnp.concatenate([real, imag], axis=1).astype(jnp.bfloat16)
    left[1, :, :depth] = jnp.concatenate([imag, -real], axis=1).astype(jnp.bfloat16)


def exchange_kernel(counts, groups, scale, bank_ref, words_hbm, gains_ref, slot_ref, *refs):
    chunks = len(counts)
    ordered_ref, total_hbm = refs[:2]
    words_bufs = refs[2 : 2 + chunks]
    send_bufs = refs[2 + chunks : 2 + 2 * chunks]
    hold_bufs = refs[2 + 2 * chunks : 2 + 3 * chunks]
    voltage, rows, total, left, gathered = refs[2 + 3 * chunks : 7 + 3 * chunks]
    word_sem, own_sem, total_sem, send_sem, recv_sem = refs[7 + 3 * chunks :]
    me = lax.axis_index("feed")
    size = lax.axis_size("feed")
    inputs = send_bufs[0].shape[2]
    bank = bank_ref[...]
    gain = gains_ref[...].astype(jnp.float32) * (1.0 / 2048.0)

    barrier = pltpu.get_barrier_semaphore()

    def greet(d, carry):
        pl.semaphore_signal(
            barrier, inc=1, device_id={"feed": (me + d) % size}, device_id_type=pl.DeviceIdType.MESH
        )
        return carry

    lax.fori_loop(1, size, greet, 0)

    def word_copy(k):
        source = words_hbm.at[pl.ds(sum(counts[:k]), counts[k] + TAPS - 1)]
        return pltpu.make_async_copy(source, words_bufs[k], word_sem.at[k])

    def own_copy(k):
        return pltpu.make_async_copy(send_bufs[k].at[me // groups], hold_bufs[k].at[me], own_sem.at[k])

    def remote(k, d):
        there = (me + d) % size
        return pltpu.make_async_remote_copy(
            src_ref=send_bufs[k].at[there // groups],
            dst_ref=hold_bufs[k].at[me],
            send_sem=send_sem.at[k, d],
            recv_sem=recv_sem.at[k, d],
            device_id={"feed": there},
            device_id_type=pl.DeviceIdType.MESH,
        )

    def channelize(k):
        words, out = words_bufs[k], send_bufs[k]
        count = counts[k]

        def block(i, carry):
            base = i * SPAN
            for m in range(SPAN + TAPS - 1):
                voltage[m * 2 * CH : (m + 1) * 2 * CH, :] = unpack(words[base + m])
            for s in range(SPAN):
                window = voltage[s * 2 * CH : (s + TAPS) * 2 * CH, :]
                parts = jnp.dot(bank, window, preferred_element_type=jnp.float32)
                whole = parts[: 2 * CH]
                for term in range(1, TERMS):
                    whole = whole + parts[2 * CH * term : 2 * CH * (term + 1)]
                real, imag = whole[:CH], whole[CH:]
                upper = gain[0] * real - gain[1] * imag
                lower = gain[0] * imag + gain[1] * real
                for lane in range(rows.shape[1]):
                    place = slice(lane * LANES, (lane + 1) * LANES)
                    rows[0, lane, s * CH : (s + 1) * CH, :] = upper[:, place]
                    rows[1, lane, s * CH : (s + 1) * CH, :] = lower[:, place]
            for c in range(CH):
                for part in range(2):
                    where = pl.ds(pl.multiple_of(part * count + base, SPAN), SPAN)
                    for lane in range(rows.shape[1]):
                        width = min(LANES, inputs - lane * LANES)
                        piece = rows[part, lane, pl.ds(c, SPAN, stride=CH), :]
                        out[c, where, lane * LANES : lane * LANES + width] = piece[:, :width].astype(
                            jnp.bfloat16
                        )
            return carry

        lax.fori_loop(0, count // SPAN, block, 0)

    def send(k):
        def one(d, carry):
            remote(k, d).start()
            return carry

        lax.fori_loop(1, size, one, 0)
        own_copy(k).start()

    def arrive(k):
        def one(d, carry):
            remote(k, d).wait_recv()
            return carry

        own_copy(k).wait()
        lax.fori_loop(1, size, one, 0)

    def drain(k):
        def one(d, carry):
            remote(k, d).wait_send()
            return carry

        lax.fori_loop(1, size, one, 0)

    for k in range(chunks):
        word_copy(k).start()
    for k in range(chunks):
        word_copy(k).wait()
        channelize(k)
        if k == 0:
            pl.semaphore_wait(barrier, size - 1)
        send(k)

    feeds = slot_ref.shape[1]
    tile = min(TILE, feeds)
    own = pl.ds(pl.multiple_of(me % groups * ROWS, ROWS), ROWS)
    for k in range(chunks - 1):
        arrive(k)
        depth = 2 * counts[k]
        set_left(left, pick(hold_bufs[k], slot_ref[:, own]), scale)

        def columns(j, carry, k=k, depth=depth):
            where = pl.ds(pl.multiple_of(j * tile, tile), tile)
            ordered = pick(hold_bufs[k], slot_ref[:, where]).astype(jnp.bfloat16)
            for part in range(2):
                product = jnp.dot(left[part, :, :depth], ordered, preferred_element_type=jnp.float32)
                if k:
                    product = product + total[part, :, where]
                total[part, :, where] = product
            return carry

        lax.fori_loop(0, feeds // tile, columns, 0)
    total_copy = pltpu.make_async_copy(total, total_hbm, total_sem)
    total_copy.start()
    last = chunks - 1

    def scatter(d, fresh):
        source = (me - d + size) % size
        arrived = hold_bufs[last][source]

        def columns(j, carry):
            where = pl.ds(pl.multiple_of(j * tile, tile), tile)
            place = lax.broadcasted_iota(jnp.int32, (inputs, tile), 0) + source * inputs
            hot = jnp.where(place == slot_ref[:, where], 1.0, 0.0).astype(jnp.bfloat16)
            part = jnp.dot(arrived, hot, preferred_element_type=jnp.float32)
            gathered[:, where] = part if fresh else gathered[:, where] + part
            return carry

        lax.fori_loop(0, feeds // tile, columns, 0)

    own_copy(last).wait()
    scatter(0, True)

    def follow(d, carry):
        remote(last, d).wait_recv()
        scatter(d, False)
        return carry

    lax.fori_loop(1, size, follow, 0)
    ordered_ref[...] = gathered[...].astype(jnp.bfloat16)
    for k in range(chunks):
        drain(k)
    total_copy.wait()


def exchange(words, gains, feed_slot, counts, inputs, groups, scale):
    size = CH * groups
    feeds = feed_slot.shape[0]
    wide = words.shape[2]
    bank = jnp.asarray(filter_bank())
    held = [jax.ShapeDtypeStruct((size, 2 * count, inputs), jnp.bfloat16) for count in counts]
    memory = pl.BlockSpec(memory_space=pltpu.VMEM)
    anywhere = pl.BlockSpec(memory_space=pl.ANY)
    chunks = len(counts)
    return pl.pallas_call(
        functools.partial(exchange_kernel, counts, groups, scale),
        out_shape=(jax.ShapeDtypeStruct((2 * counts[-1], feeds), jnp.bfloat16), jax.ShapeDtypeStruct((2, ROWS, feeds), jnp.float32)),
        in_specs=[memory, anywhere, memory, memory],
        out_specs=(memory, anywhere),
        scratch_shapes=[pltpu.VMEM((count + TAPS - 1, CH, wide), jnp.int32) for count in counts]
        + [pltpu.VMEM((CH, 2 * count, inputs), jnp.bfloat16) for count in counts]
        + [pltpu.VMEM(one.shape, one.dtype) for one in held]
        + [
            pltpu.VMEM(((SPAN + TAPS) * 2 * CH, wide), jnp.bfloat16),
            pltpu.VMEM((2, wide // LANES, SPAN * CH, LANES), jnp.float32),
            pltpu.VMEM((2, ROWS, feeds), jnp.float32),
            pltpu.VMEM((2, ROWS, 2 * max(counts)), jnp.bfloat16),
            pltpu.VMEM((2 * counts[-1], feeds), jnp.float32),
            pltpu.SemaphoreType.DMA((chunks,)),
            pltpu.SemaphoreType.DMA((chunks,)),
            pltpu.SemaphoreType.DMA,
            pltpu.SemaphoreType.DMA((chunks, size)),
            pltpu.SemaphoreType.DMA((chunks, size)),
        ],
        compiler_params=pltpu.CompilerParams(
            collective_id=0, has_side_effects=True, vmem_limit_bytes=60 * 2**20
        ),
    )(bank, words, gains, feed_slot[None])


def finish_kernel(groups, scale, whole_ref, ordered_ref, total_ref, out_ref, left):
    @pl.when(pl.program_id(0) == 0)
    def _():
        first = 0 if groups == 1 else lax.axis_index("feed") % groups * ROWS
        own = pl.ds(pl.multiple_of(first, ROWS), ROWS)
        set_left(left, whole_ref[:, own].astype(jnp.float32), scale)

    for part in range(2):
        product = jnp.dot(left[part], ordered_ref[...], preferred_element_type=jnp.float32)
        out_ref[:, part, :] = product + total_ref[part]


def finish(ordered, total, groups, scale):
    depth, feeds = ordered.shape
    tile = min(TILE, feeds)
    return pl.pallas_call(
        functools.partial(finish_kernel, groups, scale),
        out_shape=jax.ShapeDtypeStruct((ROWS, 2, feeds), jnp.float32),
        grid=(feeds // tile,),
        in_specs=[
            pl.BlockSpec((depth, feeds), lambda j: (0, 0)),
            pl.BlockSpec((depth, tile), lambda j: (0, j)),
            pl.BlockSpec((2, ROWS, tile), lambda j: (0, 0, j)),
        ],
        out_specs=pl.BlockSpec((ROWS, 2, tile), lambda j: (0, 0, j)),
        scratch_shapes=[pltpu.VMEM((2, ROWS, depth), jnp.bfloat16)],
    )(ordered, ordered, total)


def body(samples, gains, feed_slot):
    groups = lax.axis_size("feed") // CH
    inputs = samples.shape[0]
    spectra = samples.shape[2] - TAPS + 1
    counts = tuple(spectra * share // sum(SHARES) for share in SHARES)
    words = jnp.transpose(samples, (2, 1, 0))
    spare = -inputs % LANES
    if spare:
        words = jnp.pad(words, ((0, 0), (0, 0), (0, spare)))
        gains = jnp.pad(gains, ((0, 0), (0, 0), (0, spare)))
    scale = 1.0 / spectra
    ordered, total = exchange(words, gains, feed_slot, counts, inputs, groups, scale)
    return finish(ordered, total, groups, scale)


def solution(mesh):
    return jax.shard_map(
        body,
        mesh=mesh,
        in_specs=(P(("band", "feed"), None, None), P(None, "band", "feed"), P()),
        out_specs=P(("band", "feed"), None, None),
        check_vma=False,
    )
```
